32 devices in a mesh: dp: 8 (over z, y), seq: 4 (over x, core).
Axes of the slice: x: 2, y: 2, z: 4, core: 2. Of those that a mesh axis runs over, the one named last changes fastest.
Arguments:
- tokens: bfloat16 [8, 1024, 768], P('dp', 'seq'), may hold values from -6 to 6
- cotangent: bfloat16 [8, 1024, 768], P('dp', 'seq'), may hold values from -6 to 6
- lengths: int32 [8], replicated, may hold values from 256 to 1024, as said below
- slot_order: int32 [8], replicated, may hold values from 0 to 7, each once
- project_weight: bfloat16 [768, 2304], P(('dp', 'seq')), may hold values from -0.21875 to 0.21875
- output_weight: bfloat16 [768, 768], P(('dp', 'seq')), may hold values from -6 to 6
- expand_weight: bfloat16 [768, 3072], P(('dp', 'seq')), may hold values from -0.21875 to 0.21875
- reduce_weight: bfloat16 [3072, 768], P(('dp', 'seq')), may hold values from -0.109375 to 0.109375
- project_bias: bfloat16 [2304], P(('dp', 'seq')), may hold values from -3 to 3
- output_bias: bfloat16 [768], P(('dp', 'seq')), may hold values from -3 to 3
- expand_bias: bfloat16 [3072], P(('dp', 'seq')), may hold values from -3 to 3
- reduce_bias: bfloat16 [768], P(('dp', 'seq')), may hold values from -3 to 3
- first_gain: bfloat16 [768], P(('dp', 'seq')), may hold values from 0.099609375 to 1.8984375
- first_shift: bfloat16 [768], P(('dp', 'seq')), may hold values from -3 to 3
- second_gain: bfloat16 [768], P(('dp', 'seq')), may hold values from 0.099609375 to 1.8984375
- second_shift: bfloat16 [768], P(('dp', 'seq')), may hold values from -3 to 3
Outputs:
- layer_out: bfloat16 [8, 1024, 768], P('dp', 'seq')
- token_grad: float32 [8, 1024, 768], P('dp', 'seq')
- project_weight_grad: float32 [768, 2304], P(('dp', 'seq'))
- output_weight_grad: float32 [768, 768], P(('dp', 'seq'))
- expand_weight_grad: float32 [768, 3072], P(('dp', 'seq'))
- reduce_weight_grad: float32 [3072, 768], P(('dp', 'seq'))
- project_bias_grad: float32 [2304], P(('dp', 'seq'))
- output_bias_grad: float32 [768], P(('dp', 'seq'))
- expand_bias_grad: float32 [3072], P(('dp', 'seq'))
- reduce_bias_grad: float32 [768], P(('dp', 'seq'))
- first_gain_grad: float32 [768], P(('dp', 'seq'))
- first_shift_grad: float32 [768], P(('dp', 'seq'))
- second_gain_grad: float32 [768], P(('dp', 'seq'))
- second_shift_grad: float32 [768], P(('dp', 'seq'))
The draws below stay inside these ranges and needn't reach their ends.
Inputs may be any that keep to these rules, and one draw needn't show every extreme that they name: `lengths`: some sequence has 1024 valid tokens and some other has 256. `slot_order`: each sequence stands in exactly one slot.
All inputs are finite; a program needn't handle non-finite values.
Results may differ from the reference program's by a relative error of at most 0.015.
Values may be sent and summed in bfloat16 or wider, within the bound.
No kernel may reach another device: no remote copies, remote signals or barrier semaphores. Data moves between devices by JAX's collectives and lax.ppermute only.
A program may use at most 128 MiB of HBM per device.

```python
import math
import jax
import jax.numpy as jnp
from jax import lax

D = 768
H = 12
HD = 64
FF = 3072
LEN = 1024
SEQS = 8
MIN_LEN = 256


def draw_lengths(key, part):
    picked = jax.random.randint(key, (SEQS,), MIN_LEN, LEN + 1)
    target = jax.random.randint(jax.random.fold_in(key, 7), (), 0, SEQS)
    picked = picked.at[target].set(LEN)
    picked = picked.at[(target + 1) % SEQS].set(MIN_LEN)
    return picked.astype(jnp.int32)


def block_scale(own_key, dims, shards, low, largest):
    factor_of, own = 1.0, jax.random.fold_in(own_key, 6)
    for axis_at, parts in shards:
        steps = jnp.exp(jax.random.uniform(jax.random.fold_in(own, axis_at), (parts,), jnp.float32, low / len(shards), largest / len(shards)))
        factor_of = factor_of * jnp.repeat(steps, dims[axis_at] // parts).reshape([-1 if axis == axis_at else 1 for axis in range(len(dims))])
    return factor_of


def normal_values(key, shape, width, limit, split=(), kind=jnp.bfloat16):
    values = jax.random.normal(key, shape, jnp.float32) * width
    if len(split) > 0:
        values = block_scale(key, shape, split, -0.22, 0.18) * values
    return jnp.clip(values, min=-limit, max=limit).astype(kind)


def setup_inputs(seed: int = 0) -> dict:
    splits = jax.random.split(jax.random.key(seed), 17)
    return {
        "tokens": normal_values(splits[0], (SEQS, LEN, D), 1.0, 6.0, ((0, 8), (1, 4))),
        "cotangent": normal_values(splits[1], (SEQS, LEN, D), 1.0, 6.0, ((0, 8), (1, 4))),
        "lengths": draw_lengths(jax.random.fold_in(splits[16], 71), 0),
        "slot_order": jax.random.permutation(splits[3], SEQS).astype(jnp.int32),
        "project_weight": normal_values(splits[4], (D, 3 * D), D ** -0.5, 0.21875, ((0, 32),)),
        "output_weight": normal_values(splits[5], (D, D), 1.0, 6.0, ((0, 32),)),
        "expand_weight": normal_values(splits[6], (D, FF), D ** -0.5, 0.21875, ((0, 32),)),
        "reduce_weight": normal_values(splits[7], (FF, D), FF ** -0.5, 0.109375, ((0, 32),)),
        "project_bias": normal_values(splits[8], (3 * D,), 0.5, 3.0, ((0, 32),)),
        "output_bias": normal_values(splits[9], (D,), 0.5, 3.0, ((0, 32),)),
        "expand_bias": normal_values(splits[10], (FF,), 0.5, 3.0, ((0, 32),)),
        "reduce_bias": normal_values(splits[11], (D,), 0.5, 3.0, ((0, 32),)),
        "first_gain": jnp.clip(1.0 + 0.18 * jax.random.normal(splits[12], (D,), jnp.float32), 0.099609375, 1.8984375).astype(jnp.bfloat16),
        "first_shift": normal_values(splits[13], (D,), 0.5, 3.0, ((0, 32),)),
        "second_gain": jnp.clip(1.0 + 0.18 * jax.random.normal(splits[14], (D,), jnp.float32), 0.099609375, 1.8984375).astype(jnp.bfloat16),
        "second_shift": normal_values(splits[15], (D,), 0.5, 3.0, ((0, 32),)),
    }


PRECISE = lax.Precision.HIGHEST
EPSILON = 1e-12
MASKED = -1e+30

@jax.custom_vjp
def low(v):
    return lax.optimization_barrier(v.astype(jnp.bfloat16)).astype(jnp.float32)

@jax.custom_vjp
def low_back(v):
    return v

def low_keep(v):
    return (low(v), None)

def low_pass(kept, grad):
    return (grad,)

def back_keep(v):
    return (v, None)

def back_low(kept, grad):
    return (low(grad),)
low.defvjp(low_keep, low_pass)
low_back.defvjp(back_keep, back_low)

def rotate(tensor):
    lane_ids = jnp.arange(tensor.shape[-1])
    return jnp.where(lane_ids % 2 == 0, -jnp.roll(tensor, -1, axis=-1), jnp.roll(tensor, 1, axis=-1))

def angles(positions, features, head_size):
    lane_ids = jnp.arange(features)
    pair_ids = (lane_ids % head_size // 2).astype(jnp.float32)
    frequency = jnp.exp(pair_ids * (-2.0 * math.log(10000.0) / head_size))
    phases = positions.astype(jnp.float32)[:, None] * frequency[None, :]
    return (jnp.cos(phases), jnp.sin(phases))

def rotary(tensor, cosine, sine_table):
    return tensor * cosine + rotate(tensor) * sine_table

def layer_norm(tensor, gain_vec, shift_vec):
    row_mean = lax.optimization_barrier(jnp.mean(tensor, -1, keepdims=True))
    centered = tensor - row_mean
    variance = lax.optimization_barrier(jnp.mean(centered * centered, -1, keepdims=True))
    return centered * lax.rsqrt(variance + EPSILON) * gain_vec + shift_vec

def block_forward(token_rows, params, length):
    project_weight, output_weight, expand_weight, reduce_weight, project_bias, output_bias, expand_bias, reduce_bias, first_gain, first_shift, second_gain, second_shift = params
    positions = jnp.arange(LEN)
    cosine, sine_table = angles(positions, D, HD)
    key_ok = positions < length
    live_rows = key_ok.astype(jnp.float32)[:, None]
    factor = HD ** (-0.5)
    joint_rows = low_back(jnp.dot(token_rows, project_weight, precision=PRECISE) + project_bias)
    queries = low(rotary(joint_rows[:, :D], cosine, sine_table))
    key_heads = low(rotary(joint_rows[:, D:2 * D], cosine, sine_table)).reshape(LEN, H, HD)
    value_heads = low(joint_rows[:, 2 * D:]).reshape(LEN, H, HD)
    block_rows = min(512, LEN)

    def attend(row_block):
        query_heads = row_block.reshape(block_rows, H, HD)
        scores = low_back(jnp.einsum('qhd,khd->hqk', query_heads, key_heads, precision=PRECISE) * factor)
        scores = jnp.where(key_ok[None, None, :], scores, MASKED)
        row_max = lax.optimization_barrier(jnp.max(scores, -1, keepdims=True))
        log_total = row_max + jnp.log(lax.optimization_barrier(jnp.sum(jnp.exp(scores - row_max), -1, keepdims=True)))
        softmax = low(jnp.exp(scores - log_total))
        return jnp.einsum('hqk,khd->qhd', softmax, value_heads, precision=PRECISE).reshape(block_rows, D)
    mixture = lax.map(jax.checkpoint(attend), queries.reshape(LEN // block_rows, block_rows, D)).reshape(LEN, D)
    attended = low_back(low(mixture))
    branch = low_back(jnp.dot(attended, output_weight, precision=PRECISE) + output_bias)
    normed_one = layer_norm(token_rows + branch, first_gain, first_shift)
    hidden = low_back(jnp.dot(low(normed_one), expand_weight, precision=PRECISE) + expand_bias)
    activated = low(jax.nn.gelu(hidden, approximate=False))
    branch_two = low_back(jnp.dot(activated, reduce_weight, precision=PRECISE) + reduce_bias)
    return layer_norm(normed_one + branch_two, second_gain, second_shift) * live_rows

def reference(tokens, cotangent, lengths, slot_order, project_weight, output_weight, expand_weight, reduce_weight, project_bias, output_bias, expand_bias, reduce_bias, first_gain, first_shift, second_gain, second_shift):
    params = tuple((tensor.astype(jnp.float32) for tensor in (project_weight, output_weight, expand_weight, reduce_weight, project_bias, output_bias, expand_bias, reduce_bias, first_gain, first_shift, second_gain, second_shift)))
    slot_lengths = lengths[slot_order]

    def accumulate(totals, sequence):
        row_block, back_rows, length = sequence

        def forward_one(token_rows, weights_in):
            return block_forward(token_rows, weights_in, length)
        layer_rows, pull_back = jax.vjp(forward_one, row_block.astype(jnp.float32), params)
        row_grads, param_grads = pull_back(back_rows.astype(jnp.float32))
        totals = jax.tree.map(jnp.add, totals, param_grads)
        return (totals, (layer_rows.astype(jnp.bfloat16), row_grads))
    initial = tuple((jnp.zeros(tensor.shape, jnp.float32) for tensor in params))
    totals, (outputs, row_grads) = lax.scan(accumulate, initial, (tokens, cotangent, slot_lengths))
    return (outputs, row_grads, totals[0], totals[1], totals[2], totals[3], totals[4], totals[5], totals[6], totals[7], totals[8], totals[9], totals[10], totals[11])
```

```python
from functools import partial
import math

import jax
import jax.numpy as jnp
from jax import lax
from jax.experimental import pallas as pl
from jax.experimental.pallas import tpu as pltpu
from jax.sharding import PartitionSpec as P

HD = 64


EPSILON = 1e-12
MASKED = -1e30


def rotate(tensor):
    lane_ids = jnp.arange(tensor.shape[-1])
    return jnp.where(
        lane_ids % 2 == 0, -jnp.roll(tensor, -1, axis=-1), jnp.roll(tensor, 1, axis=-1)
    )


def angles(positions, features, head_size):
    lane_ids = jnp.arange(features)
    pair_ids = (lane_ids % head_size // 2).astype(jnp.float32)
    frequency = jnp.exp(pair_ids * (-2.0 * math.log(10000.0) / head_size))
    phases = positions.astype(jnp.float32)[:, None] * frequency[None, :]
    return (jnp.cos(phases), jnp.sin(phases))


def rotary(tensor, cosine, sine_table):
    return tensor * cosine + rotate(tensor) * sine_table


def rotary_back(grad_in, cosine, sine_table):
    return grad_in * cosine - rotate(grad_in * sine_table)


def layer_norm(tensor, gain_vec, shift_vec):
    row_mean = jnp.mean(tensor, -1, keepdims=True)
    centered = tensor - row_mean
    variance = jnp.mean(centered * centered, -1, keepdims=True)
    return centered * lax.rsqrt(variance + EPSILON) * gain_vec + shift_vec


def contract_rows(left_op, right_op):
    return lax.dot_general(
        left_op, right_op, (((0,), (0,)), ((), ())), preferred_element_type=jnp.float32
    )


def times_transpose(left_op, right_op):
    return lax.dot_general(
        left_op, right_op, (((1,), (1,)), ((), ())), preferred_element_type=jnp.float32
    )


def score_block(query_heads, key_rows, begin_at, seq_len, factor):
    batches, block_len, features = key_rows.shape
    key_heads = key_rows.reshape(batches, block_len, query_heads.shape[2], HD)
    scores = (
        jnp.einsum("bqhd,bkhd->bhqk", query_heads, key_heads, preferred_element_type=jnp.float32)
        * factor
    )
    places = begin_at + jnp.arange(block_len)
    key_ok = places[None, :] < seq_len[:, None]
    return jnp.where(key_ok[:, None, None, :], scores, MASKED)


def softmax_stats(query_heads, key_all, seq_len, factor, block_len):
    batches, span_len, head_count, head_size = query_heads.shape
    block_count = key_all.shape[1] // block_len

    def softmax_visit_block(carried, block_index):
        running_max, running_sum = carried
        begin_at = block_index * block_len
        scores = score_block(
            query_heads,
            lax.dynamic_slice_in_dim(key_all, begin_at, block_len, 1),
            begin_at,
            seq_len,
            factor,
        )
        new_max = jnp.maximum(running_max, jnp.max(scores, -1))
        running_sum = running_sum * jnp.exp(running_max - new_max) + jnp.sum(
            jnp.exp(scores - new_max[..., None]), -1
        )
        return ((new_max, running_sum), None)

    initial = (
        jnp.full((batches, head_count, span_len), MASKED, jnp.float32),
        jnp.zeros((batches, head_count, span_len), jnp.float32),
    )
    (running_max, running_sum), _ = lax.scan(softmax_visit_block, initial, jnp.arange(block_count))
    return running_max + jnp.log(running_sum)


def attend_values(query_heads, key_all, value_all, seq_len, logsum, factor, block_len):
    batches, span_len, head_count, head_size = query_heads.shape
    block_count = key_all.shape[1] // block_len

    def attend_visit_block(accumulated, block_index):
        begin_at = block_index * block_len
        scores = score_block(
            query_heads,
            lax.dynamic_slice_in_dim(key_all, begin_at, block_len, 1),
            begin_at,
            seq_len,
            factor,
        )
        softmax = jnp.exp(scores - logsum[..., None]).astype(jnp.bfloat16)
        value_heads = lax.dynamic_slice_in_dim(value_all, begin_at, block_len, 1).reshape(
            batches, block_len, head_count, HD
        )
        return (
            accumulated
            + jnp.einsum(
                "bhqk,bkhd->bqhd", softmax, value_heads, preferred_element_type=jnp.float32
            ),
            None,
        )

    initial = jnp.zeros((batches, span_len, head_count, HD), jnp.float32)
    accumulated, _ = lax.scan(attend_visit_block, initial, jnp.arange(block_count))
    return accumulated


def grad_offsets(query_heads, grad_heads, key_all, value_all, seq_len, logsum, factor, block_len):
    batches, span_len, head_count, head_size = query_heads.shape
    block_count = key_all.shape[1] // block_len

    def grad_visit_block(accumulated, block_index):
        begin_at = block_index * block_len
        scores = score_block(
            query_heads,
            lax.dynamic_slice_in_dim(key_all, begin_at, block_len, 1),
            begin_at,
            seq_len,
            factor,
        )
        softmax = jnp.exp(scores - logsum[..., None])
        value_heads = lax.dynamic_slice_in_dim(value_all, begin_at, block_len, 1).reshape(
            batches, block_len, head_count, HD
        )
        prob_grads = jnp.einsum(
            "bqhd,bkhd->bhqk", grad_heads, value_heads, preferred_element_type=jnp.float32
        )
        return (accumulated + jnp.sum(softmax * prob_grads, -1), None)

    initial = jnp.zeros((batches, head_count, span_len), jnp.float32)
    accumulated, _ = lax.scan(grad_visit_block, initial, jnp.arange(block_count))
    return accumulated


def key_pass(
    query_heads, grad_heads, key_all, value_all, seq_len, logsum, offsets, factor, block_len
):
    batches, span_len, head_count, head_size = query_heads.shape
    total_len, features = (key_all.shape[1], key_all.shape[2])
    block_count = total_len // block_len

    def key_visit_block(carried, block_index):
        grad_query, grad_key, grad_value = carried
        begin_at = block_index * block_len
        key_rows = lax.dynamic_slice_in_dim(key_all, begin_at, block_len, 1)
        scores = score_block(query_heads, key_rows, begin_at, seq_len, factor)
        softmax = jnp.exp(scores - logsum[..., None])
        value_heads = lax.dynamic_slice_in_dim(value_all, begin_at, block_len, 1).reshape(
            batches, block_len, head_count, HD
        )
        prob_grads = jnp.einsum(
            "bqhd,bkhd->bhqk", grad_heads, value_heads, preferred_element_type=jnp.float32
        )
        score_grads = (softmax * (prob_grads - offsets[..., None])).astype(jnp.bfloat16)
        key_heads = key_rows.reshape(batches, block_len, head_count, HD)
        grad_query = (
            grad_query
            + jnp.einsum(
                "bhqk,bkhd->bqhd", score_grads, key_heads, preferred_element_type=jnp.float32
            )
            * factor
        )
        key_part = (
            jnp.einsum(
                "bhqk,bqhd->bkhd", score_grads, query_heads, preferred_element_type=jnp.float32
            )
            * factor
        )
        value_part = jnp.einsum(
            "bhqk,bqhd->bkhd",
            softmax.astype(jnp.bfloat16),
            grad_heads,
            preferred_element_type=jnp.float32,
        )
        grad_key = lax.dynamic_update_slice_in_dim(
            grad_key, key_part.reshape(batches, block_len, features), begin_at, 1
        )
        grad_value = lax.dynamic_update_slice_in_dim(
            grad_value, value_part.reshape(batches, block_len, features), begin_at, 1
        )
        return ((grad_query, grad_key, grad_value), None)

    key_zeros = jnp.zeros((batches, total_len, features), jnp.float32)
    initial = (jnp.zeros((batches, span_len, head_count, HD), jnp.float32), key_zeros, key_zeros)
    carried, _ = lax.scan(key_visit_block, initial, jnp.arange(block_count))
    return carried


def body_general(
    tokens,
    cotangent,
    lengths,
    slot_order,
    project_weight,
    output_weight,
    expand_weight,
    reduce_weight,
    project_bias,
    output_bias,
    expand_bias,
    reduce_bias,
    first_gain,
    first_shift,
    second_gain,
    second_shift,
):
    params = (
        lax.all_gather(project_weight, ("dp", "seq"), axis=0, tiled=True),
        lax.all_gather(output_weight, ("dp", "seq"), axis=0, tiled=True),
        lax.all_gather(expand_weight, ("dp", "seq"), axis=0, tiled=True),
        lax.all_gather(reduce_weight, ("dp", "seq"), axis=0, tiled=True),
        lax.all_gather(project_bias, ("dp", "seq"), axis=0, tiled=True),
        lax.all_gather(output_bias, ("dp", "seq"), axis=0, tiled=True),
        lax.all_gather(expand_bias, ("dp", "seq"), axis=0, tiled=True),
        lax.all_gather(reduce_bias, ("dp", "seq"), axis=0, tiled=True),
        lax.all_gather(first_gain, ("dp", "seq"), axis=0, tiled=True),
        lax.all_gather(first_shift, ("dp", "seq"), axis=0, tiled=True),
        lax.all_gather(second_gain, ("dp", "seq"), axis=0, tiled=True),
        lax.all_gather(second_shift, ("dp", "seq"), axis=0, tiled=True),
    )
    batches, span_len, features = tokens.shape
    head_count = features // HD
    factor = HD ** (-0.5)
    rows_count = batches * span_len
    seq_total = lengths.shape[0]
    slot_ids = lax.axis_index("dp") * batches + jnp.arange(batches)
    slot_match = slot_ids[:, None] == jnp.arange(seq_total)[None, :]
    chosen = jnp.sum(jnp.where(slot_match, slot_order[None, :], 0), 1)
    seq_len = jnp.sum(
        jnp.where(chosen[:, None] == jnp.arange(seq_total)[None, :], lengths[None, :], 0), 1
    )
    positions = lax.axis_index("seq") * span_len + jnp.arange(span_len)
    cosine, sine_table = angles(positions, features, HD)
    key_ok = positions[None, :] < seq_len[:, None]
    live_rows = key_ok.astype(jnp.float32).reshape(rows_count, 1)
    proj_w, out_w, exp_w, red_w = (params[0], params[1], params[2], params[3])
    proj_b, out_b, exp_b, red_b = [vector.astype(jnp.float32) for vector in params[4:8]]
    gain_one, shift_one, gain_two, shift_two = [
        vector.astype(jnp.float32) for vector in params[8:12]
    ]
    token_rows = tokens.reshape(rows_count, features)
    joint_rows = (jnp.dot(token_rows, proj_w, preferred_element_type=jnp.float32) + proj_b).reshape(
        batches, span_len, 3 * features
    )
    query_rot = rotary(joint_rows[..., :features], cosine, sine_table).astype(jnp.bfloat16)
    key_rot = rotary(joint_rows[..., features : 2 * features], cosine, sine_table).astype(
        jnp.bfloat16
    )
    value_low = joint_rows[..., 2 * features :].astype(jnp.bfloat16)
    key_all, value_all = (
        lax.all_gather(key_rot, "seq", axis=1, tiled=True),
        lax.all_gather(value_low, "seq", axis=1, tiled=True),
    )
    block_len = min(512, key_all.shape[1])
    query_heads = query_rot.reshape(batches, span_len, head_count, HD)
    logsum = softmax_stats(query_heads, key_all, seq_len, factor, block_len)
    mixture = attend_values(query_heads, key_all, value_all, seq_len, logsum, factor, block_len)
    attended = mixture.reshape(rows_count, features).astype(jnp.bfloat16)
    resid_one = (
        token_rows.astype(jnp.float32)
        + jnp.dot(attended, out_w, preferred_element_type=jnp.float32)
        + out_b
    )
    normed_one = layer_norm(resid_one, gain_one, shift_one)
    normed_low = normed_one.astype(jnp.bfloat16)
    hidden = jnp.dot(normed_low, exp_w, preferred_element_type=jnp.float32) + exp_b
    activated = jax.nn.gelu(hidden, approximate=False).astype(jnp.bfloat16)
    resid_two = normed_one + jnp.dot(activated, red_w, preferred_element_type=jnp.float32) + red_b
    layer_out = (layer_norm(resid_two, gain_two, shift_two) * live_rows).astype(jnp.bfloat16)
    params = (
        lax.all_gather(project_weight, ("dp", "seq"), axis=0, tiled=True),
        lax.all_gather(output_weight, ("dp", "seq"), axis=0, tiled=True),
        lax.all_gather(expand_weight, ("dp", "seq"), axis=0, tiled=True),
        lax.all_gather(reduce_weight, ("dp", "seq"), axis=0, tiled=True),
        lax.all_gather(project_bias, ("dp", "seq"), axis=0, tiled=True),
        lax.all_gather(output_bias, ("dp", "seq"), axis=0, tiled=True),
        lax.all_gather(expand_bias, ("dp", "seq"), axis=0, tiled=True),
        lax.all_gather(reduce_bias, ("dp", "seq"), axis=0, tiled=True),
        lax.all_gather(first_gain, ("dp", "seq"), axis=0, tiled=True),
        lax.all_gather(first_shift, ("dp", "seq"), axis=0, tiled=True),
        lax.all_gather(second_gain, ("dp", "seq"), axis=0, tiled=True),
        lax.all_gather(second_shift, ("dp", "seq"), axis=0, tiled=True),
    )
    proj_w, out_w, exp_w, red_w = (params[0], params[1], params[2], params[3])
    gain_one, shift_one, gain_two, shift_two = [
        vector.astype(jnp.float32) for vector in params[8:12]
    ]
    seed_grad = cotangent.reshape(rows_count, features).astype(jnp.float32) * live_rows
    _, pull_two = jax.vjp(layer_norm, resid_two, gain_two, shift_two)
    grad_two, grad_gain_two, grad_shift_two = pull_two(seed_grad)
    grad_two_low = grad_two.astype(jnp.bfloat16)
    grad_reduce = contract_rows(activated, grad_two_low)
    grad_reduce_bias = jnp.sum(grad_two_low.astype(jnp.float32), 0)
    grad_act = times_transpose(grad_two_low, red_w)
    _, pull_gelu = jax.vjp(partial(jax.nn.gelu, approximate=False), hidden)
    grad_hidden = pull_gelu(grad_act)[0].astype(jnp.bfloat16)
    grad_expand = contract_rows(normed_low, grad_hidden)
    grad_expand_bias = jnp.sum(grad_hidden.astype(jnp.float32), 0)
    grad_normed = grad_two + times_transpose(grad_hidden, exp_w)
    _, pull_one = jax.vjp(layer_norm, resid_one, gain_one, shift_one)
    grad_one, grad_gain_one, grad_shift_one = pull_one(grad_normed)
    grad_one_low = grad_one.astype(jnp.bfloat16)
    grad_output = contract_rows(attended, grad_one_low)
    grad_output_bias = jnp.sum(grad_one_low.astype(jnp.float32), 0)
    grad_mixture = times_transpose(grad_one_low, out_w).astype(jnp.bfloat16)
    grad_heads = grad_mixture.reshape(batches, span_len, head_count, HD)
    offsets = grad_offsets(
        query_heads, grad_heads, key_all, value_all, seq_len, logsum, factor, block_len
    )
    grad_query, key_terms, value_terms = key_pass(
        query_heads, grad_heads, key_all, value_all, seq_len, logsum, offsets, factor, block_len
    )
    grad_key, grad_value = (
        lax.psum_scatter(
            key_terms.astype(jnp.bfloat16), "seq", scatter_dimension=1, tiled=True
        ).astype(jnp.float32),
        lax.psum_scatter(
            value_terms.astype(jnp.bfloat16), "seq", scatter_dimension=1, tiled=True
        ).astype(jnp.float32),
    )
    grad_query = rotary_back(grad_query.reshape(batches, span_len, features), cosine, sine_table)
    grad_key = rotary_back(grad_key, cosine, sine_table)
    grad_joint = (
        jnp.concatenate([grad_query, grad_key, grad_value], -1)
        .reshape(rows_count, 3 * features)
        .astype(jnp.bfloat16)
    )
    grad_project = contract_rows(token_rows, grad_joint)
    grad_project_bias = jnp.sum(grad_joint.astype(jnp.float32), 0)
    token_grad = grad_one + times_transpose(grad_joint, proj_w)
    owned_grads = (
        lax.psum_scatter(grad_project, ("dp", "seq"), scatter_dimension=0, tiled=True),
        lax.psum_scatter(grad_output, ("dp", "seq"), scatter_dimension=0, tiled=True),
        lax.psum_scatter(grad_expand, ("dp", "seq"), scatter_dimension=0, tiled=True),
        lax.psum_scatter(grad_reduce, ("dp", "seq"), scatter_dimension=0, tiled=True),
        lax.psum_scatter(grad_project_bias, ("dp", "seq"), scatter_dimension=0, tiled=True),
        lax.psum_scatter(grad_output_bias, ("dp", "seq"), scatter_dimension=0, tiled=True),
        lax.psum_scatter(grad_expand_bias, ("dp", "seq"), scatter_dimension=0, tiled=True),
        lax.psum_scatter(grad_reduce_bias, ("dp", "seq"), scatter_dimension=0, tiled=True),
        lax.psum_scatter(grad_gain_one, ("dp", "seq"), scatter_dimension=0, tiled=True),
        lax.psum_scatter(grad_shift_one, ("dp", "seq"), scatter_dimension=0, tiled=True),
        lax.psum_scatter(grad_gain_two, ("dp", "seq"), scatter_dimension=0, tiled=True),
        lax.psum_scatter(grad_shift_two, ("dp", "seq"), scatter_dimension=0, tiled=True),
    )
    return (
        layer_out.reshape(batches, span_len, features),
        token_grad.reshape(batches, span_len, features),
        owned_grads[0],
        owned_grads[1],
        owned_grads[2],
        owned_grads[3],
        owned_grads[4],
        owned_grads[5],
        owned_grads[6],
        owned_grads[7],
        owned_grads[8],
        owned_grads[9],
        owned_grads[10],
        owned_grads[11],
    )


ALL = ("dp", "seq")
SEQ = 4
DP = 8
SMALL = 13
PIECE = 640
QROWS = 256


def splits_heads(mesh):
    return mesh.shape["dp"] == DP and mesh.shape["seq"] == SEQ


def xor_send(tensor, mask, count):
    return lax.ppermute(tensor, ALL, [(i, i ^ mask) for i in range(count)])


def take(tensor, index, axis):
    return lax.dynamic_index_in_dim(tensor, index, axis, keepdims=False)


def attention_forward_kernel(
    x_ref, w_ref, bias_ref, cos_ref, sin_a_ref, sin_b_ref, mask_ref, q_ref, k_ref, v_ref, att_ref
):
    rows_count = x_ref.shape[0]
    heads = q_ref.shape[0]
    width = heads * HD
    qk_width = 2 * width
    copies = qk_width // cos_ref.shape[1]

    def project(block, carry):
        rows = pl.ds(pl.multiple_of(block * QROWS, QROWS), QROWS)
        joint = (
            jnp.dot(x_ref[rows, :], w_ref[...], preferred_element_type=jnp.float32) + bias_ref[...]
        )
        both = joint[:, :qk_width]
        cosine = jnp.concatenate([cos_ref[rows, :]] * copies, -1)
        sin_a = jnp.concatenate([sin_a_ref[rows, :]] * copies, -1)
        sin_b = jnp.concatenate([sin_b_ref[rows, :]] * copies, -1)
        both = (
            both * cosine
            + pltpu.roll(both, qk_width - 1, 1) * sin_a
            + pltpu.roll(both, 1, 1) * sin_b
        )
        queries = (both[:, :width] * HD ** (-0.5)).astype(jnp.bfloat16)
        keys = both[:, width:].astype(jnp.bfloat16)
        values = joint[:, qk_width : qk_width + width].astype(jnp.bfloat16)
        for head in range(heads):
            lanes = slice(head * HD, (head + 1) * HD)
            q_ref[head, rows, :] = queries[:, lanes]
            k_ref[head, rows, :] = keys[:, lanes]
            v_ref[head, rows, :] = values[:, lanes]
        return carry

    lax.fori_loop(0, rows_count // QROWS, project, 0)

    def attend(block, carry):
        rows = pl.ds(pl.multiple_of(block * QROWS, QROWS), QROWS)
        mixed = []
        for head in range(heads):
            scores = times_transpose(q_ref[head, rows, :], k_ref[head]) + mask_ref[...]
            row_max = jnp.max(scores, -1, keepdims=True)
            exps = jnp.exp(scores - row_max)
            row_sum = jnp.sum(exps, -1, keepdims=True)
            mixture = jnp.dot(
                exps.astype(jnp.bfloat16), v_ref[head], preferred_element_type=jnp.float32
            )
            mixed.append(mixture / row_sum)
        att_ref[rows, :] = jnp.concatenate(mixed, -1).astype(jnp.bfloat16)
        return carry

    lax.fori_loop(0, rows_count // QROWS, attend, 0)


def attention_backward_kernel(
    q_ref,
    k_ref,
    v_ref,
    go_ref,
    mask_ref,
    cos_ref,
    sin_a_ref,
    sin_b_ref,
    gj_ref,
    dq_ref,
    dk_ref,
    dv_ref,
):
    heads, rows_count, _ = q_ref.shape
    width = heads * HD
    qk_width = 2 * width
    copies = qk_width // cos_ref.shape[1]
    dk_ref[...] = jnp.zeros_like(dk_ref)
    dv_ref[...] = jnp.zeros_like(dv_ref)

    def visit(block, carry):
        rows = pl.ds(pl.multiple_of(block * QROWS, QROWS), QROWS)
        grads = go_ref[rows, :]
        for head in range(heads):
            grad_head = grads[:, head * HD : (head + 1) * HD]
            query = q_ref[head, rows, :]
            scores = times_transpose(k_ref[head], query) + mask_ref[...]
            exps = jnp.exp(scores - jnp.max(scores, 0, keepdims=True))
            probs = exps * (1.0 / jnp.sum(exps, 0, keepdims=True))
            prob_grads = times_transpose(v_ref[head], grad_head)
            offsets = jnp.sum(probs * prob_grads, 0, keepdims=True)
            score_grads = (probs * (prob_grads - offsets)).astype(jnp.bfloat16)
            dv_ref[head] += jnp.dot(
                probs.astype(jnp.bfloat16), grad_head, preferred_element_type=jnp.float32
            )
            dk_ref[head] += jnp.dot(score_grads, query, preferred_element_type=jnp.float32)
            dq_ref[head, rows, :] = contract_rows(score_grads, k_ref[head])
        return carry

    lax.fori_loop(0, rows_count // QROWS, visit, 0)

    def finish(block, carry):
        rows = pl.ds(pl.multiple_of(block * QROWS, QROWS), QROWS)
        both = jnp.concatenate(
            [dq_ref[head, rows, :] * HD ** (-0.5) for head in range(heads)]
            + [dk_ref[head, rows, :] for head in range(heads)],
            -1,
        )
        cosine = jnp.concatenate([cos_ref[rows, :]] * copies, -1)
        sin_a = jnp.concatenate([sin_a_ref[rows, :]] * copies, -1)
        sin_b = jnp.concatenate([sin_b_ref[rows, :]] * copies, -1)
        both = (
            both * cosine
            + pltpu.roll(both * sin_b, qk_width - 1, 1)
            + pltpu.roll(both * sin_a, 1, 1)
        )
        values = jnp.concatenate([dv_ref[head, rows, :] for head in range(heads)], -1)
        gj_ref[rows, :] = jnp.concatenate([both, values], -1).astype(jnp.bfloat16)
        return carry

    lax.fori_loop(0, rows_count // QROWS, finish, 0)


VMEM_SPEC = pl.BlockSpec(memory_space=pltpu.VMEM)


def call_in_vmem(kernel, operands, outs, scratch, flops, exps):
    touched = sum(a.size * a.dtype.itemsize for a in operands) + sum(
        math.prod(o.shape) * o.dtype.itemsize for o in outs
    )
    return pl.pallas_call(
        kernel,
        out_shape=outs,
        in_specs=[VMEM_SPEC] * len(operands),
        out_specs=[VMEM_SPEC] * len(outs),
        scratch_shapes=scratch,
        compiler_params=pltpu.CompilerParams(vmem_limit_bytes=50 * 2**20),
        cost_estimate=pl.CostEstimate(
            flops=flops, transcendentals=exps, bytes_accessed=touched
        ),
    )(*operands)


def reduce_tree(part, place, count, order):
    block = part.shape[1:]
    bits = {"core": 1, "x": 2, "y": 4}
    done = []
    arranged = part.reshape((count // 8, 2, 2, 2) + block)
    axis_of = {"y": 1, "x": 2, "core": 3}
    for name in order:
        axis = axis_of[name] - sum(axis_of[d] < axis_of[name] for d in done)
        mine = (place // bits[name]) % 2
        other = xor_send(take(arranged, 1 - mine, axis), bits[name], count)
        arranged = take(arranged, mine, axis) + other
        done.append(name)
    far = place // 8
    total = take(arranged, far, 0).astype(jnp.float32)
    for step in range(1, count // 8):
        other = xor_send(take(arranged, far ^ step, 0), 8 * step, count)
        total = total + other.astype(jnp.float32)
    return total


def body_heads(
    tokens,
    cotangent,
    lengths,
    slot_order,
    project_weight,
    output_weight,
    expand_weight,
    reduce_weight,
    project_bias,
    output_bias,
    expand_bias,
    reduce_bias,
    first_gain,
    first_shift,
    second_gain,
    second_shift,
):
    count = DP * SEQ
    _, span_len, features = tokens.shape
    seq_total = lengths.shape[0]
    total_len = SEQ * span_len
    hidden_size = expand_weight.shape[1]
    row_share = features // count
    hidden_share = hidden_size // count
    width = features // SEQ
    heads = width // HD
    here = lax.axis_index("seq")
    place = lax.axis_index("dp") * SEQ + here
    f32, bf16 = jnp.float32, jnp.bfloat16

    columns = hidden_size // features
    packed = jnp.concatenate(
        [reduce_weight]
        + [expand_weight[:, k * features : (k + 1) * features] for k in range(columns)]
        + [output_weight],
        0,
    )
    gathered = lax.all_gather(packed, ALL, axis=0, tiled=False)

    own_rows = tokens.reshape(span_len, features)
    far_rows = xor_send(own_rows, 2, count)
    near = xor_send(jnp.stack([own_rows, far_rows]), 1, count)
    sequence_rows = jnp.concatenate([own_rows, near[0], far_rows, near[1]], 0)

    vectors = jnp.concatenate(
        [
            project_bias,
            output_bias,
            expand_bias,
            reduce_bias,
            first_gain,
            first_shift,
            second_gain,
            second_shift,
        ]
    ).reshape(row_share, SMALL)
    by_heads = project_weight.reshape(row_share, 3, SEQ, width).transpose(2, 0, 1, 3)
    by_heads = by_heads.reshape(SEQ, row_share, 3 * width)
    piece = jnp.concatenate(
        [
            by_heads,
            jnp.broadcast_to(vectors, (SEQ, row_share, SMALL)),
            jnp.zeros((SEQ, row_share, PIECE - 3 * width - SMALL), bf16),
        ],
        -1,
    )
    pieces = jnp.broadcast_to(piece, (DP, SEQ, row_share, PIECE)).reshape(count, row_share, PIECE)
    pieces = lax.all_to_all(pieces, ALL, 0, 0, tiled=True)
    proj_w = pieces.reshape(features, PIECE)
    vectors = pieces[:, :, 3 * width : 3 * width + SMALL].reshape(count, row_share * SMALL)
    vectors = vectors.astype(f32)
    proj_b, out_b, exp_b, red_b, gain_one, shift_one, gain_two, shift_two = [
        part.reshape(-1)
        for part in jnp.split(
            vectors,
            [
                3 * row_share,
                4 * row_share,
                4 * row_share + hidden_share,
                5 * row_share + hidden_share,
                6 * row_share + hidden_share,
                7 * row_share + hidden_share,
                8 * row_share + hidden_share,
            ],
            1,
        )
    ]
    head_bias = take(proj_b.reshape(3, SEQ, width), here, 1).reshape(1, 3 * width)
    head_bias = jnp.concatenate([head_bias, jnp.zeros((1, PIECE - 3 * width), f32)], -1)

    slot = lax.axis_index("dp")
    chosen = jnp.sum(jnp.where(jnp.arange(seq_total) == slot, slot_order, 0))
    seq_len = jnp.sum(jnp.where(jnp.arange(seq_total) == chosen, lengths, 0))
    blocks = here ^ jnp.arange(SEQ)
    positions = (blocks[:, None] * span_len + jnp.arange(span_len)[None, :]).reshape(total_len)
    lane_ids = jnp.arange(2 * HD)
    cosine, sine_table = angles(positions, 2 * HD, HD)
    even = lane_ids % 2 == 0
    sin_a = jnp.where(even, -sine_table, 0.0)
    sin_b = jnp.where(even, 0.0, sine_table)
    mask = jnp.where(positions < seq_len, 0.0, MASKED)
    live_rows = (positions[:span_len] < seq_len).astype(f32)[:, None]

    head_type = jax.ShapeDtypeStruct((heads, total_len, HD), bf16)
    scores_count = heads * total_len * total_len
    queries, keys, values, mixed = call_in_vmem(
        attention_forward_kernel,
        (sequence_rows, proj_w, head_bias, cosine, sin_a, sin_b, mask[None, :]),
        (head_type, head_type, head_type, jax.ShapeDtypeStruct((total_len, width), bf16)),
        (),
        2 * total_len * features * PIECE + 4 * scores_count * HD,
        scores_count,
    )
    mixed = mixed.reshape(SEQ, span_len, width)
    attended = jnp.concatenate(
        [mixed[0]] + [xor_send(mixed[r], r, count) for r in range(1, SEQ)], -1
    )

    out_all = gathered[:, hidden_share + columns * row_share :].reshape(SEQ, width, features)
    out_w = jnp.concatenate([take(out_all, here ^ r, 0) for r in range(SEQ)], 0)
    exp_w = [
        gathered[:, hidden_share + k * row_share : hidden_share + (k + 1) * row_share].reshape(
            features, features
        )
        for k in range(columns)
    ]
    red_w = gathered[:, :hidden_share].reshape(hidden_size, features)

    resid_one = own_rows.astype(f32) + jnp.dot(attended, out_w, preferred_element_type=f32) + out_b
    normed_one = layer_norm(resid_one, gain_one, shift_one)
    normed_low = normed_one.astype(bf16)
    hidden = [
        jnp.dot(normed_low, exp_w[k], preferred_element_type=f32)
        + exp_b[k * features : (k + 1) * features]
        for k in range(columns)
    ]
    activated = jnp.concatenate(
        [jax.nn.gelu(h, approximate=False).astype(bf16) for h in hidden], -1
    )
    resid_two = normed_one + jnp.dot(activated, red_w, preferred_element_type=f32) + red_b
    layer_out = (layer_norm(resid_two, gain_two, shift_two) * live_rows).astype(bf16)

    seed_grad = cotangent.reshape(span_len, features).astype(f32) * live_rows
    _, pull_two = jax.vjp(layer_norm, resid_two, gain_two, shift_two)
    grad_two, grad_gain_two, grad_shift_two = pull_two(seed_grad)
    grad_two_low = grad_two.astype(bf16)
    grad_hidden, grad_normed = [], grad_two
    for k in range(columns):
        grad_act = times_transpose(grad_two_low, red_w[k * features : (k + 1) * features])
        _, pull_gelu = jax.vjp(partial(jax.nn.gelu, approximate=False), hidden[k])
        grad_hidden.append(pull_gelu(grad_act)[0].astype(bf16))
        grad_normed = grad_normed + times_transpose(grad_hidden[k], exp_w[k])
    _, pull_one = jax.vjp(layer_norm, resid_one, gain_one, shift_one)
    grad_one, grad_gain_one, grad_shift_one = pull_one(grad_normed)
    grad_one_low = grad_one.astype(bf16)
    grad_mixed = times_transpose(grad_one_low, out_w).astype(bf16)
    grad_mixed = [grad_mixed[:, r * width : (r + 1) * width] for r in range(SEQ)]
    grad_heads = jnp.concatenate(
        [grad_mixed[0]] + [xor_send(grad_mixed[r], r, count) for r in range(1, SEQ)], 0
    )

    red_part = contract_rows(activated, grad_two_low).astype(bf16)
    red_part = red_part.reshape(count, hidden_share, features)
    exp_part = [
        contract_rows(normed_low, g).astype(bf16).reshape(count, row_share, features)
        for g in grad_hidden
    ]
    out_part = contract_rows(attended, grad_one_low).astype(bf16).reshape(SEQ, width, features)
    out_part = jnp.concatenate([take(out_part, here ^ r, 0) for r in range(SEQ)], 0)
    out_part = out_part.reshape(count, row_share, features)
    red_grad = reduce_tree(red_part, place, count, ("core", "y", "x"))
    rest_grad = reduce_tree(
        jnp.concatenate(exp_part + [out_part], 1), place, count, ("core", "x", "y")
    )
    exp_grad = jnp.concatenate(
        [rest_grad[k * row_share : (k + 1) * row_share] for k in range(columns)], -1
    )
    out_grad = rest_grad[columns * row_share :]

    (grad_joint,) = call_in_vmem(
        attention_backward_kernel,
        (queries, keys, values, grad_heads, mask[:, None], cosine, sin_a, sin_b),
        (jax.ShapeDtypeStruct((total_len, 3 * width), bf16),),
        [pltpu.VMEM((heads, total_len, HD), f32)] * 3,
        10 * scores_count * HD,
        scores_count,
    )
    proj_part = contract_rows(sequence_rows, grad_joint).astype(bf16)
    bias_part = jnp.sum(grad_joint.astype(f32), 0).reshape(3, 1, width)
    bias_part = jnp.where(
        jnp.arange(SEQ)[None, :, None] == here, bias_part, 0.0
    ).reshape(count, 3 * row_share)
    vector_part = jnp.concatenate(
        [bias_part]
        + [
            part.reshape(count, -1)
            for part in (
                jnp.sum(grad_one_low.astype(f32), 0),
                jnp.concatenate([jnp.sum(g.astype(f32), 0) for g in grad_hidden]),
                jnp.sum(grad_two_low.astype(f32), 0),
                grad_gain_one,
                grad_shift_one,
                grad_gain_two,
                grad_shift_two,
            )
        ],
        1,
    ).astype(bf16)
    piece = jnp.concatenate(
        [
            proj_part.reshape(count, row_share, 3 * width),
            vector_part.reshape(count, row_share, SMALL),
            jnp.zeros((count, row_share, PIECE - 3 * width - SMALL), bf16),
        ],
        -1,
    )
    pieces = lax.all_to_all(piece, ALL, 0, 0, tiled=True)
    summed = jnp.sum(pieces.reshape(DP, SEQ, row_share, PIECE).astype(f32), 0)
    proj_grad = summed[:, :, : 3 * width].reshape(SEQ, row_share, 3, width)
    proj_grad = proj_grad.transpose(1, 2, 0, 3).reshape(row_share, 3 * features)
    vector_grad = jnp.sum(summed[:, :, 3 * width : 3 * width + SMALL], 0)
    vector_grad = jnp.split(
        vector_grad.reshape(row_share * SMALL),
        [
            3 * row_share,
            4 * row_share,
            4 * row_share + hidden_share,
            5 * row_share + hidden_share,
            6 * row_share + hidden_share,
            7 * row_share + hidden_share,
            8 * row_share + hidden_share,
        ],
    )

    token_part = times_transpose(grad_joint, proj_w[:, : 3 * width])
    token_part = token_part.reshape(SEQ, span_len, features)
    near = xor_send(jnp.stack([token_part[1], token_part[3]]).astype(bf16), 1, count)
    far = xor_send((token_part[2] + near[1].astype(f32)).astype(bf16), 2, count)
    token_grad = grad_one + token_part[0] + near[0].astype(f32) + far.astype(f32)
    return (
        layer_out.reshape(1, span_len, features),
        token_grad.reshape(1, span_len, features),
        proj_grad,
        out_grad,
        exp_grad,
        red_grad,
        *vector_grad,
    )


def solution(mesh):
    chosen = body_heads if splits_heads(mesh) else body_general
    in_specs = (
        P("dp", "seq", None),
        P("dp", "seq", None),
        P(),
        P(),
        P(("dp", "seq"), None),
        P(("dp", "seq"), None),
        P(("dp", "seq"), None),
        P(("dp", "seq"), None),
        P(("dp", "seq")),
        P(("dp", "seq")),
        P(("dp", "seq")),
        P(("dp", "seq")),
        P(("dp", "seq")),
        P(("dp", "seq")),
        P(("dp", "seq")),
        P(("dp", "seq")),
    )
    out_specs = (
        P("dp", "seq", None),
        P("dp", "seq", None),
        P(("dp", "seq"), None),
        P(("dp", "seq"), None),
        P(("dp", "seq"), None),
        P(("dp", "seq"), None),
        P(("dp", "seq")),
        P(("dp", "seq")),
        P(("dp", "seq")),
        P(("dp", "seq")),
        P(("dp", "seq")),
        P(("dp", "seq")),
        P(("dp", "seq")),
        P(("dp", "seq")),
    )
    return jax.shard_map(chosen, mesh=mesh, in_specs=in_specs, out_specs=out_specs, check_vma=False)
```
